32 devices in a mesh: group: 2 (over y), seq: 4 (over z), head: 4 (over x, core).
Axes of the slice: x: 2, y: 2, z: 4, core: 2. Of those that a mesh axis runs over, the one named last changes fastest.
Arguments:
- queries: bfloat16 [2048, 64, 128], P(('group', 'seq'), 'head'), parts along dimension 0, may hold values from -6 to 6
- key_states: bfloat16 [2048, 8, 128], P(('group', 'seq'), 'head'), parts along dimension 0, may hold values from -6 to 6
- value_states: bfloat16 [2048, 8, 128], P(('group', 'seq'), 'head'), parts along dimension 0, may hold values from -6 to 6
- grad_output: bfloat16 [2048, 64, 128], P(('group', 'seq'), 'head'), parts along dimension 0, may hold values from -6 to 6
- block_list: int32 [16, 6], P(('group', 'seq')), parts along dimension 0, may hold values from 0 to 7, as said below
- visible_count: int32 [16], P(('group', 'seq')), parts along dimension 0, may hold values from 1 to 6, as said below
Outputs:
- attn_out: bfloat16 [2048, 64, 128], P(('group', 'seq'), 'head'), parts along dimension 0
- grad_queries: bfloat16 [2048, 64, 128], P(('group', 'seq'), 'head'), parts along dimension 0
- grad_keys: bfloat16 [2048, 8, 128], P(('group', 'seq'), 'head'), parts along dimension 0
- grad_values: bfloat16 [2048, 8, 128], P(('group', 'seq'), 'head'), parts along dimension 0
The draws below stay inside these ranges and needn't reach their ends.
There are 2 independent parts, one for each index of `group`. The reference program is written for one: setup_inputs(seed, part) draws one part's arguments, and reference() takes and returns one part's arrays. A program takes and returns all parts, laid end to end along the dimension named above; each array names one. Nothing has to cross between parts.
Inputs may be any that keep to these rules, and one draw needn't show every extreme that they name: Row b of block_list: entry 0 is b; entries 1 to visible_count[b] - 1 are distinct blocks among b - 31 to b - 1 ; the remaining entries repeat b. `visible_count`: some row reaches 6.
All inputs are finite; a program needn't handle non-finite values.
Results may differ from the reference program's by a relative error of at most 0.022.
Values may be sent and summed in bfloat16 or wider, within the bound.
A program may use at most 128 MiB of HBM per device.

```python
import math
import jax
import jax.numpy as jnp
from jax import lax

HEAD_DIM = 128
Q_HEADS = 64
KV_HEADS = 8
BLOCK = 128
WIN_BLOCKS = 32
MAXVIS = 6
TOKENS = 1024
QBLOCKS = 8


def agent_lists(key):
    block_ids = jnp.arange(QBLOCKS, dtype=jnp.int32)
    agent_ids = jax.random.randint(jax.random.fold_in(key, 11), (QBLOCKS,), 1, 4).astype(jnp.int32)
    agent_ids = jnp.where(block_ids % 3 == 0, 0, agent_ids)
    offsets = jnp.arange(1, WIN_BLOCKS, dtype=jnp.int32)
    earlier = block_ids[:, None] - offsets[None, :]
    inside = earlier >= 0
    earlier_safe = jnp.maximum(earlier, 0)
    earlier_agent = agent_ids[earlier_safe]
    own_agent = agent_ids[:, None]
    allowed = inside & ((earlier_agent == 0) | (earlier_agent == own_agent) | (own_agent == 0))
    ranking = jax.random.randint(jax.random.fold_in(key, 12), earlier.shape, 0, 1 << 20).astype(jnp.int32) * WIN_BLOCKS + offsets[None, :]
    ranking = jnp.where(allowed, ranking, -1)
    best_values, best_slots = lax.top_k(ranking, MAXVIS - 1)
    chosen = jnp.take_along_axis(earlier_safe, best_slots, axis=1)
    budget = jax.random.randint(jax.random.fold_in(key, 13), (QBLOCKS,), 1, MAXVIS).astype(jnp.int32)
    budget = jnp.where(block_ids % 3 == 0, MAXVIS - 1, budget)
    live = (best_values >= 0) & (jnp.arange(MAXVIS - 1, dtype=jnp.int32)[None, :] < budget[:, None])
    chosen = jnp.where(live, chosen, block_ids[:, None])
    lists = jnp.concatenate([block_ids[:, None], chosen], axis=1).astype(jnp.int32)
    counts = (1 + jnp.sum(live.astype(jnp.int32), axis=1)).astype(jnp.int32)
    return (lists, counts)


def draw_block_list(key, part):
    return agent_lists(key)[0]


def draw_visible_count(key, part):
    return agent_lists(key)[1]


def draw_queries(key, part):
    shape = (TOKENS, Q_HEADS, HEAD_DIM)
    base = jnp.clip(jax.random.normal(jax.random.fold_in(key, 41), shape, jnp.float32), -6.0, 6.0)
    return base.astype(jnp.bfloat16)


def draw_key_states(key, part):
    shape = (TOKENS, KV_HEADS, HEAD_DIM)
    base = jnp.clip(jax.random.normal(jax.random.fold_in(key, 42), shape, jnp.float32), -6.0, 6.0)
    return base.astype(jnp.bfloat16)


def level_of(stream_key, dims, split, least, top_value):
    loudness = 1.0
    for axis_at, blocks in split:
        steps = jax.random.uniform(jax.random.fold_in(jax.random.fold_in(stream_key, 6), axis_at), (blocks,), jnp.float32, least / len(split), top_value / len(split))
        loudness = loudness * jnp.repeat(jnp.exp(steps), dims[axis_at] // blocks).reshape((-1,) + (1,) * (len(dims) - 1 - axis_at))
    return loudness


def gaussian(rng, extent, width, most, split=(), kind=jnp.bfloat16):
    result = width * jax.random.normal(rng, extent, jnp.float32)
    if split:
        result = result * level_of(rng, extent, split, -0.22, 0.18)
    return jnp.clip(result, -most, most).astype(kind)


def setup_inputs(seed: int = 0, part: int = 0) -> dict:
    keys = jax.random.split(jax.random.key(seed), 7)
    part_splits = jax.random.split(jax.random.fold_in(keys[6], part), 7)
    queries = draw_queries(jax.random.fold_in(jax.random.fold_in(keys[6], part), 71), part)
    key_states = draw_key_states(jax.random.fold_in(jax.random.fold_in(keys[6], part), 71), part)
    value_states = gaussian(part_splits[2], (TOKENS, KV_HEADS, HEAD_DIM), 1.0, 6.0, ((0, 4), (1, 4)))
    grad_output = gaussian(part_splits[3], (TOKENS, Q_HEADS, HEAD_DIM), 1.0, 6.0, ((0, 4), (1, 4)))
    block_list = draw_block_list(jax.random.fold_in(jax.random.fold_in(keys[6], part), 71), part)
    visible_count = draw_visible_count(jax.random.fold_in(jax.random.fold_in(keys[6], part), 71), part)
    return {"queries": queries, "key_states": key_states, "value_states": value_states, "grad_output": grad_output, "block_list": block_list, "visible_count": visible_count}


def reference(queries, key_states, value_states, grad_output, block_list, visible_count):
    group_size = Q_HEADS // KV_HEADS
    score_scale = 1.0 / math.sqrt(HEAD_DIM)
    query_grid = queries.reshape(QBLOCKS, BLOCK, KV_HEADS, group_size, HEAD_DIM)
    gradout_grid = grad_output.reshape(QBLOCKS, BLOCK, KV_HEADS, group_size, HEAD_DIM)
    key_grid = key_states.reshape(QBLOCKS, BLOCK, KV_HEADS, HEAD_DIM)
    value_grid = value_states.reshape(QBLOCKS, BLOCK, KV_HEADS, HEAD_DIM)
    positions = jnp.arange(BLOCK)
    causal = positions[None, :] <= positions[:, None]
    slots = jnp.arange(MAXVIS)

    def step(carried, inputs):
        grad_key_acc, grad_value_acc = carried
        block_index, query_blk, gradout_blk, picked, live_count = inputs
        key_sel = key_grid[picked].astype(jnp.float32)
        value_sel = value_grid[picked].astype(jnp.float32)
        query_full = query_blk.astype(jnp.float32)
        gradout_full = gradout_blk.astype(jnp.float32)
        slot_live = slots < live_count
        diagonal = picked == block_index
        visible = slot_live[None, :, None] & (jnp.logical_not(diagonal)[None, :, None] | causal[:, None, :])
        scores = jnp.einsum('rhgd,skhd->hgrsk', query_full, key_sel) * score_scale
        scores = jnp.where(visible, scores, -1e+30)
        row_top = lax.optimization_barrier(jnp.max(scores, axis=(3, 4), keepdims=True))
        weights = jnp.exp(scores - row_top)
        row_total = lax.optimization_barrier(jnp.sum(weights, axis=(3, 4), keepdims=True))
        weights_bf = lax.optimization_barrier(weights.astype(jnp.bfloat16))
        mixed_rows = jnp.einsum('hgrsk,skhd->rhgd', weights_bf.astype(jnp.float32), value_sel)
        norm_total = jnp.transpose(row_total[:, :, :, 0, 0], (2, 0, 1))[..., None]
        out_blk = (mixed_rows / norm_total).astype(jnp.bfloat16)
        log_total = row_top + jnp.log(row_total)
        row_delta = lax.optimization_barrier(jnp.sum(gradout_full * out_blk.astype(jnp.float32), axis=-1))
        row_delta = jnp.transpose(row_delta, (1, 2, 0))[..., None, None]
        prob_full = jnp.exp(scores - log_total)
        prob_bf = lax.optimization_barrier(prob_full.astype(jnp.bfloat16))
        grad_prob = jnp.einsum('rhgd,skhd->hgrsk', gradout_full, value_sel)
        grad_score = lax.optimization_barrier((prob_full * (grad_prob - row_delta)).astype(jnp.bfloat16))
        grad_score_full = grad_score.astype(jnp.float32)
        grad_query_blk = (jnp.einsum('hgrsk,skhd->rhgd', grad_score_full, key_sel) * score_scale).astype(jnp.bfloat16)
        key_part = jnp.einsum('hgrsk,rhgd->skhd', grad_score_full, query_full) * score_scale
        value_part = jnp.einsum('hgrsk,rhgd->skhd', prob_bf.astype(jnp.float32), gradout_full)
        grad_key_acc = grad_key_acc.at[picked].add(key_part)
        grad_value_acc = grad_value_acc.at[picked].add(value_part)
        return ((grad_key_acc, grad_value_acc), (out_blk, grad_query_blk))
    initial = (jnp.zeros(key_grid.shape, jnp.float32), jnp.zeros(value_grid.shape, jnp.float32))
    inputs = (jnp.arange(QBLOCKS, dtype=jnp.int32), query_grid, gradout_grid, block_list, visible_count)
    (grad_key_acc, grad_value_acc), (out_blocks, grad_query_blocks) = lax.scan(step, initial, inputs)
    attn_out = out_blocks.reshape(TOKENS, Q_HEADS, HEAD_DIM)
    grad_queries = grad_query_blocks.reshape(TOKENS, Q_HEADS, HEAD_DIM)
    grad_keys = grad_key_acc.reshape(TOKENS, KV_HEADS, HEAD_DIM).astype(jnp.bfloat16)
    grad_values = grad_value_acc.reshape(TOKENS, KV_HEADS, HEAD_DIM).astype(jnp.bfloat16)
    return (attn_out, grad_queries, grad_keys, grad_values)
```

```python
from functools import partial
import math

import jax
import jax.numpy as jnp
from jax import lax
from jax.experimental import pallas as pl
from jax.experimental.pallas import tpu as pltpu
from jax.sharding import PartitionSpec as P

BLOCK = 128
REACH = 16
FAR = -1e30
CHUNK = 512


def from_behind(block, axis, distance):
    devices = range(lax.axis_size(axis))
    route = [(i - distance, i) for i in devices if i - distance in devices]
    return lax.ppermute(block, axis, route)


def pick_blocks(blocks, at):
    return jnp.concatenate(
        [lax.dynamic_slice_in_dim(blocks, at[s], 1, 0) for s in range(at.shape[0])], 0
    )


def block_step(carried, inputs, key_blocks, value_blocks, base_block, score_scale):
    grad_key_win, grad_value_win = carried
    block_index, query_blk, gradout_blk, picked, live_count = inputs
    local_blocks = picked - base_block
    key_sel = pick_blocks(key_blocks, local_blocks)
    value_sel = pick_blocks(value_blocks, local_blocks)
    positions = jnp.arange(query_blk.shape[0])
    causal = positions[None, :] <= positions[:, None]
    slot_live = jnp.arange(picked.shape[0]) < live_count
    diagonal = picked == block_index
    visible = slot_live[None, :, None] & (
        jnp.logical_not(diagonal)[None, :, None] | causal[:, None, :]
    )
    scores = (
        jnp.einsum("rhgd,skhd->hgrsk", query_blk, key_sel, preferred_element_type=jnp.float32)
        * score_scale
    )
    scores = jnp.where(visible, scores, -1e30)
    row_top = jnp.max(scores, axis=(3, 4), keepdims=True)
    weights = jnp.exp(scores - row_top)
    row_total = jnp.sum(weights, axis=(3, 4), keepdims=True)
    mixed_rows = jnp.einsum(
        "hgrsk,skhd->rhgd",
        weights.astype(jnp.bfloat16),
        value_sel,
        preferred_element_type=jnp.float32,
    )
    norm_total = jnp.transpose(row_total[:, :, :, 0, 0], (2, 0, 1))[..., None]
    out_blk = (mixed_rows / norm_total).astype(jnp.bfloat16)
    log_total = row_top + jnp.log(row_total)
    row_delta = jnp.sum(gradout_blk.astype(jnp.float32) * out_blk.astype(jnp.float32), axis=-1)
    row_delta = jnp.transpose(row_delta, (1, 2, 0))[..., None, None]
    prob_full = jnp.exp(scores - log_total)
    prob_bf = prob_full.astype(jnp.bfloat16)
    grad_prob = jnp.einsum(
        "rhgd,skhd->hgrsk", gradout_blk, value_sel, preferred_element_type=jnp.float32
    )
    grad_score = (prob_full * (grad_prob - row_delta)).astype(jnp.bfloat16)
    grad_query_blk = (
        jnp.einsum("hgrsk,skhd->rhgd", grad_score, key_sel, preferred_element_type=jnp.float32)
        * score_scale
    ).astype(jnp.bfloat16)
    key_part = (
        jnp.einsum("hgrsk,rhgd->skhd", grad_score, query_blk, preferred_element_type=jnp.float32)
        * score_scale
    )
    value_part = jnp.einsum(
        "hgrsk,rhgd->skhd", prob_bf, gradout_blk, preferred_element_type=jnp.float32
    )
    grad_key_win = grad_key_win.at[local_blocks].add(key_part)
    grad_value_win = grad_value_win.at[local_blocks].add(value_part)
    return ((grad_key_win, grad_value_win), (out_blk, grad_query_blk))


def body(queries, key_states, value_states, grad_output, block_list, visible_count):
    tok_dev, kv_dev, head_dim = key_states.shape
    q_dev = queries.shape[1]
    group_size = q_dev // kv_dev
    blocks_dev = tok_dev // BLOCK
    seq_size = lax.axis_size("seq")
    seq_index = lax.axis_index("seq")
    reachable = min(REACH, seq_size - 1)
    score_scale = 1.0 / math.sqrt(head_dim)
    key_parts = []
    value_parts = []
    for distance in range(REACH, 0, -1):
        if distance <= reachable:
            far_keys, far_values = from_behind((key_states, value_states), "seq", distance)
        else:
            far_keys = jnp.zeros_like(key_states)
            far_values = jnp.zeros_like(value_states)
        key_parts.append(far_keys)
        value_parts.append(far_values)
    key_window = jnp.concatenate(key_parts + [key_states], 0)
    value_window = jnp.concatenate(value_parts + [value_states], 0)
    key_blocks = key_window.reshape((REACH + 1) * blocks_dev, BLOCK, kv_dev, head_dim)
    value_blocks = value_window.reshape((REACH + 1) * blocks_dev, BLOCK, kv_dev, head_dim)
    base_block = (seq_index - REACH) * blocks_dev
    block_ids = seq_index * blocks_dev + jnp.arange(blocks_dev, dtype=jnp.int32)
    query_grid = queries.reshape(blocks_dev, BLOCK, kv_dev, group_size, head_dim)
    gradout_grid = grad_output.reshape(blocks_dev, BLOCK, kv_dev, group_size, head_dim)
    initial = (jnp.zeros(key_blocks.shape, jnp.float32), jnp.zeros(value_blocks.shape, jnp.float32))
    stepper = partial(
        block_step,
        key_blocks=key_blocks,
        value_blocks=value_blocks,
        base_block=base_block,
        score_scale=score_scale,
    )
    (grad_key_win, grad_value_win), (out_blocks, grad_query_blocks) = lax.scan(
        stepper, initial, (block_ids, query_grid, gradout_grid, block_list, visible_count)
    )
    attn_out = out_blocks.reshape(tok_dev, q_dev, head_dim)
    grad_queries = grad_query_blocks.reshape(tok_dev, q_dev, head_dim)
    key_segments = grad_key_win.reshape(REACH + 1, tok_dev, kv_dev, head_dim)
    value_segments = grad_value_win.reshape(REACH + 1, tok_dev, kv_dev, head_dim)
    grad_keys = key_segments[REACH]
    grad_values = value_segments[REACH]
    for distance in range(1, reachable + 1):
        back_keys, back_values = from_behind(
            (key_segments[REACH - distance], value_segments[REACH - distance]), "seq", -distance
        )
        grad_keys = grad_keys + back_keys
        grad_values = grad_values + back_values
    return (
        attn_out,
        grad_queries,
        grad_keys.astype(jnp.bfloat16),
        grad_values.astype(jnp.bfloat16),
    )


NT = (((1,), (1,)), ((), ()))
NN = (((1,), (0,)), ((), ()))


def dot(a, b, dims):
    return lax.dot_general(a, b, dims, preferred_element_type=jnp.float32)


def layer_kernel(
    n,
    list_ref,
    count_ref,
    q_in,
    do_in,
    k_in,
    v_in,
    out_ref,
    dq_ref,
    dk_ref,
    dv_ref,
    bias,
    q_ref,
    do_ref,
    k_raw,
    v_raw,
    io_sems,
    kall,
    vall,
    kt,
    vt,
    qs,
    dos,
    wide,
    prob,
    score_grad,
    tops,
    sums,
    factor,
    delta,
    out_t,
    dq_t,
    dk_own,
    dv_own,
    dk_send,
    dv_send,
    dk_recv,
    dv_recv,
    dv_mid,
    k_sems,
    v_sems,
    dk_sems,
    dv_sems,
    mid_sems,
):
    z = lax.axis_index("seq")
    last = n - 1
    barrier = pltpu.get_barrier_semaphore()

    @pl.when(z > 0)
    def _():
        pl.semaphore_signal(barrier, inc=1, device_id={"seq": z - 1})

    @pl.when(z < last)
    def _():
        pl.semaphore_signal(barrier, inc=1, device_id={"seq": z + 1})

    k_copy = pltpu.make_async_copy(k_in, k_raw, io_sems.at[0])
    v_copy = pltpu.make_async_copy(v_in, v_raw, io_sems.at[1])
    q_copy = pltpu.make_async_copy(q_in, q_ref, io_sems.at[2])
    do_copy = pltpu.make_async_copy(do_in, do_ref, io_sems.at[3])
    k_copy.start()
    q_copy.start()
    v_copy.start()
    do_copy.start()
    _, kv, tok, dim = kall.shape
    group = q_ref.shape[1] // kv
    blocks = tok // BLOCK
    rows = tok * group
    chunks = rows // CHUNK
    block_rows = BLOCK * group
    scale = 1.0 / math.sqrt(dim)
    scale2 = scale * math.log2(math.e)

    def hop(held, sems, h, d):
        return pltpu.make_async_remote_copy(
            src_ref=held.at[d, h],
            dst_ref=held.at[d + 1, h],
            send_sem=sems.at[0, d, h],
            recv_sem=sems.at[1, d, h],
            device_id={"seq": z + 1},
        )

    def k_hop(h, d):
        return hop(kall, k_sems, h, d)

    def v_hop(h, d):
        return hop(vall, v_sems, h, d)

    def back(send, recv, sems, h, d):
        return pltpu.make_async_remote_copy(
            src_ref=send.at[d - 1, h],
            dst_ref=recv.at[d - 1, h],
            send_sem=sems.at[0, d - 1, h],
            recv_sem=sems.at[1, d - 1, h],
            device_id={"seq": z - d},
        )

    def mid_back(h, d):
        return pltpu.make_async_remote_copy(
            src_ref=dv_send.at[d - 1, h],
            dst_ref=dv_mid.at[d - 2, h],
            send_sem=mid_sems.at[0, d - 2, h],
            recv_sem=mid_sems.at[1, d - 2, h],
            device_id={"seq": z - 1},
        )

    def dk_back(h, d):
        return back(dk_send, dk_recv, dk_sems, h, d)

    def dv_back(h, d):
        return back(dv_send, dv_recv, dv_sems, h, d)

    def split_heads(src, dst, dst_t):
        full = src[...].astype(jnp.float32)
        for h in range(kv):
            part = full[:, h, :]
            dst[0, h] = part.astype(jnp.bfloat16)

    for b in range(blocks):
        for d in range(n):
            for j in range(blocks):
                c = (z - d) * blocks + j
                hits = jnp.int32(0)
                for s in range(list_ref.shape[1]):
                    live = jnp.logical_and(list_ref[b, s] == c, s < count_ref[b])
                    hits = jnp.where(live, jnp.int32(1), hits)
                bias[b, d * blocks + j] = jnp.where(hits > 0, jnp.float32(0.0), jnp.float32(FAR))

    k_copy.wait()
    split_heads(k_raw, kall, kt)

    inner = jnp.logical_and(z > 0, z < last)

    @pl.when(inner)
    def _():
        pl.semaphore_wait(barrier, 2)

    @pl.when(jnp.logical_not(inner))
    def _():
        pl.semaphore_wait(barrier, 1)

    @pl.when(z < last)
    def _():
        k_hop(0, 0).start()

    @pl.when(z == 0)
    def _():
        k_hop(1, 0).start()

    v_copy.wait()
    split_heads(v_raw, vall, vt)

    tops[...] = jnp.full(tops.shape, FAR, jnp.float32)
    sums[...] = jnp.zeros(sums.shape, jnp.float32)
    delta[...] = jnp.zeros(delta.shape, jnp.float32)

    step_tok = CHUNK // group

    def regroup_from(src, dst):
        def step(i, _):
            at = pl.ds(pl.multiple_of(i * step_tok, step_tok), step_tok)
            to = pl.ds(pl.multiple_of(i * CHUNK, CHUNK), CHUNK)
            full = src[at].astype(jnp.float32)
            for h in range(kv):
                part = full[:, h * group : (h + 1) * group, :]
                dst[h, to, :] = part.reshape(CHUNK, dim).astype(jnp.bfloat16)
            return 0

        lax.fori_loop(0, tok // step_tok, step, 0)

    def lanes(c):
        return slice(c * CHUNK, (c + 1) * CHUNK)

    def keys_of(d):
        return slice(d * tok, (d + 1) * tok)

    def score_unit(h, d):
        keys = kall[d, h]
        for c in range(chunks):
            b = c * CHUNK // block_rows
            s = dot(keys, qs[h, lanes(c), :], NT) * scale2
            parts = []
            for j in range(blocks):
                sj = s[j * BLOCK : (j + 1) * BLOCK]
                if d == 0 and j > b:
                    sj = jnp.full(sj.shape, FAR, jnp.float32)
                elif d == 0 and j == b:
                    first = (c * CHUNK - b * block_rows) // group
                    p_at = lax.broadcasted_iota(jnp.int32, sj.shape, 0)
                    t_at = first + lax.broadcasted_iota(jnp.int32, sj.shape, 1) // group
                    sj = jnp.where(p_at <= t_at, sj, FAR)
                else:
                    sj = sj + bias[b, d * blocks + j]
                parts.append(sj)
            s = jnp.concatenate(parts, 0)
            top = jnp.max(s, axis=0, keepdims=True)
            w = jnp.exp2(s - top)
            tops[d, h, :, lanes(c)] = top
            sums[d, h, :, lanes(c)] = jnp.sum(w, axis=0, keepdims=True)
            wide[d, h, :, lanes(c)] = w

    def factors(h):
        top = tops[0, h]
        for d in range(1, n):
            top = jnp.maximum(top, tops[d, h])
        grow = [jnp.exp2(tops[d, h] - top) for d in range(n)]
        total = sum(grow[d] * sums[d, h] for d in range(n))
        for d in range(n):
            factor[d, h] = grow[d] / total

    def prob_unit(h, d):
        acc = jnp.zeros((tok, dim), jnp.float32)
        for c in range(chunks):
            p = (wide[d, h, :, lanes(c)] * factor[d, h, :, lanes(c)]).astype(jnp.bfloat16)
            prob[h, keys_of(d), lanes(c)] = p
            acc = acc + dot(p, dos[h, lanes(c), :], NN)
        return acc

    def value_unit(h, d):
        values = vall[d, h]
        vt[h, :, keys_of(d)] = values.astype(jnp.float32).T.astype(jnp.bfloat16)
        for c in range(chunks):
            p = prob[h, keys_of(d), lanes(c)]
            gp = dot(values, dos[h, lanes(c), :], NT)
            wide[d, h, :, lanes(c)] = gp
            delta[h, :, lanes(c)] += jnp.sum(p.astype(jnp.float32) * gp, axis=0, keepdims=True)

    def grad_unit(h, d):
        acc = jnp.zeros((tok, dim), jnp.float32)
        for c in range(chunks):
            p = prob[h, keys_of(d), lanes(c)].astype(jnp.float32)
            gs = p * (wide[d, h, :, lanes(c)] - delta[h, :, lanes(c)])
            gs = gs.astype(jnp.bfloat16)
            score_grad[h, keys_of(d), lanes(c)] = gs
            acc = acc + dot(gs, qs[h, lanes(c), :], NN)
        return acc * scale

    def mix_unit(h, left, right, dst, k):
        span = (k + 1) * tok
        for c in range(chunks):
            dst[h, :, lanes(c)] = dot(left[h, :, :span], right[h, :span, lanes(c)], NN)

    def arrive(hop_of, h, d, then):
        if d > 0:
            hop_of(h, d - 1).wait_recv()
        if 0 < d < last:

            @pl.when(z < last)
            def _():
                hop_of(h, d).start()

        if then is not None and d < last:

            @pl.when(z == d)
            def _():
                then()

    def score_head(h):
        for d in range(n):

            @pl.when(z >= d)
            def _(d=d):
                if h == 0 and d > 0:
                    arrive(k_hop, h, d, lambda: k_hop(1, 0).start())
                elif h == 1:
                    arrive(k_hop, h, d, lambda: v_hop(0, 0).start())
                score_unit(h, d)

        factors(h)

    def prob_head(h):
        for d in range(last, 0, -1):

            @pl.when(z >= d)
            def _(d=d):
                acc = prob_unit(h, d)

                @pl.when(z == last - 1)
                def _():
                    dv_own[d, h] = acc

                @pl.when(z != last - 1)
                def _():
                    dv_send[d - 1, h] = acc.astype(jnp.bfloat16)

                if d == 1:

                    @pl.when(z != last - 1)
                    def _():
                        dv_back(h, d).start()

                else:

                    @pl.when(z == last)
                    def _():
                        mid_back(h, d).start()

                    @pl.when(z < last - 1)
                    def _():
                        dv_back(h, d).start()

    def mid_head(h):
        @pl.when(z == last - 1)
        def _():
            for d in range(last - 1, 0, -1):
                mid_back(h, d + 1).wait_recv()
                both = dv_own[d, h] + dv_mid[d - 1, h].astype(jnp.float32)
                dv_send[d - 1, h] = both.astype(jnp.bfloat16)
                dv_back(h, d).start()

    def value_head(h):
        for d in range(n):

            @pl.when(z >= d)
            def _(d=d):
                if h == 0:
                    arrive(v_hop, h, d, lambda: v_hop(1, 0).start())
                else:
                    arrive(v_hop, h, d, None)
                value_unit(h, d)

    def grad_head(h):
        for d in range(last, 0, -1):

            @pl.when(z >= d)
            def _(d=d):
                dk_send[d - 1, h] = grad_unit(h, d).astype(jnp.bfloat16)
                dk_back(h, d).start()

    def mix_head(h, left, right, dst):
        for k in range(n):

            @pl.when(z == k)
            def _(k=k):
                mix_unit(h, left, right, dst, k)

    def key_turns(h):
        for d in range(n):

            @pl.when(z >= d)
            def _(d=d):
                kt[h, :, keys_of(d)] = kall[d, h].astype(jnp.float32).T.astype(jnp.bfloat16)

    q_copy.wait()
    regroup_from(q_ref, qs)
    score_head(0)
    do_copy.wait()
    regroup_from(do_ref, dos)
    prob_head(0)
    score_head(1)
    prob_head(1)
    for h in range(kv):
        dv_own[0, h] = prob_unit(h, 0)
    value_head(0)
    mid_head(0)
    grad_head(0)
    value_head(1)
    grad_head(1)
    mid_head(1)
    for h in range(kv):
        dk_own[0, h] = grad_unit(h, 0)

    def untwist(src, dst, factor_out):
        for i in range(tok // step_tok):
            heads = []
            for h in range(kv):
                x = src[h, :, i * CHUNK : (i + 1) * CHUNK].T
                heads.append(x.reshape(step_tok, group, dim))
            full = jnp.concatenate(heads, 1) * factor_out
            dst[i * step_tok : (i + 1) * step_tok] = full.astype(jnp.bfloat16)

    for h in range(kv):
        mix_head(h, vt, prob, out_t)
    untwist(out_t, q_ref, 1.0)
    out_copy = pltpu.make_async_copy(q_ref, out_ref, io_sems.at[4])
    out_copy.start()
    for h in range(kv):
        key_turns(h)
        mix_head(h, kt, score_grad, dq_t)
    untwist(dq_t, do_ref, scale)
    dq_copy = pltpu.make_async_copy(do_ref, dq_ref, io_sems.at[5])
    dq_copy.start()

    for e in range(1, n):

        @pl.when(z + e <= last)
        def _(e=e):
            for h in range(kv):

                @pl.when(jnp.logical_or(e == 1, z + e < last))
                def _():
                    dv_back(h, e).wait_recv()
                    dv_own[0, h] += dv_recv[e - 1, h].astype(jnp.float32)

                dk_back(h, e).wait_recv()
                dk_own[0, h] += dk_recv[e - 1, h].astype(jnp.float32)

    dv_ref[...] = dv_own[0].astype(jnp.bfloat16)
    dk_ref[...] = dk_own[0].astype(jnp.bfloat16)

    for d in range(n - 1):

        @pl.when(jnp.logical_and(z >= d, z < last))
        def _(d=d):
            for h in range(kv):
                k_hop(h, d).wait_send()
                v_hop(h, d).wait_send()

    for d in range(1, n):

        @pl.when(z >= d)
        def _(d=d):
            for h in range(kv):
                dk_back(h, d).wait_send()
                if d == 1:
                    dv_back(h, d).wait_send()
                else:

                    @pl.when(z == last)
                    def _():
                        mid_back(h, d).wait_send()

                    @pl.when(z < last)
                    def _():
                        dv_back(h, d).wait_send()

    out_copy.wait()
    dq_copy.wait()


def write_kernel(out_in, dq_in, dk_in, dv_in, out_ref, dq_ref, dk_ref, dv_ref):
    out_ref[...] = out_in[...]
    dq_ref[...] = dq_in[...]
    for src, dst in ((dk_in, dk_ref), (dv_in, dv_ref)):
        full = src[...].astype(jnp.float32)
        dst[...] = jnp.stack([full[h] for h in range(full.shape[0])], axis=1).astype(jnp.bfloat16)


def short_body(queries, key_states, value_states, grad_output, block_list, visible_count):
    n = lax.axis_size("seq")
    tok, kv, dim = key_states.shape
    group = queries.shape[1] // kv
    rows = tok * group
    blocks = tok // BLOCK
    shard = (kv, tok, dim)
    vmem = pl.BlockSpec(memory_space=pltpu.VMEM)
    smem = pl.BlockSpec(memory_space=pltpu.SMEM)
    hbm = pl.BlockSpec(memory_space=pl.ANY)
    f32, bf16 = jnp.float32, jnp.bfloat16
    hops = pltpu.SemaphoreType.DMA((2, n - 1, kv))
    parts = pltpu.VMEM((n - 1, *shard), bf16)
    out, dq, dk, dv = pl.pallas_call(
        partial(layer_kernel, n),
        out_shape=(
            jax.ShapeDtypeStruct(queries.shape, bf16),
            jax.ShapeDtypeStruct(queries.shape, bf16),
            jax.ShapeDtypeStruct(shard, bf16),
            jax.ShapeDtypeStruct(shard, bf16),
        ),
        in_specs=[smem, smem, hbm, hbm, hbm, hbm],
        out_specs=(hbm, hbm, vmem, vmem),
        scratch_shapes=[
            pltpu.SMEM((blocks, n * blocks), f32),
            pltpu.VMEM(queries.shape, bf16),
            pltpu.VMEM(queries.shape, bf16),
            pltpu.VMEM(key_states.shape, bf16),
            pltpu.VMEM(key_states.shape, bf16),
            pltpu.SemaphoreType.DMA((6,)),
            pltpu.VMEM((n, *shard), bf16),
            pltpu.VMEM((n, *shard), bf16),
            pltpu.VMEM((kv, dim, n * tok), bf16),
            pltpu.VMEM((kv, dim, n * tok), bf16),
            pltpu.VMEM((kv, rows, dim), bf16),
            pltpu.VMEM((kv, rows, dim), bf16),
            pltpu.VMEM((n, kv, tok, rows), f32),
            pltpu.VMEM((kv, n * tok, rows), bf16),
            pltpu.VMEM((kv, n * tok, rows), bf16),
            pltpu.VMEM((n, kv, 1, rows), f32),
            pltpu.VMEM((n, kv, 1, rows), f32),
            pltpu.VMEM((n, kv, 1, rows), f32),
            pltpu.VMEM((kv, 1, rows), f32),
            pltpu.VMEM((kv, dim, rows), f32),
            pltpu.VMEM((kv, dim, rows), f32),
            pltpu.VMEM((1, *shard), f32),
            pltpu.VMEM((n, *shard), f32),
            parts,
            parts,
            parts,
            parts,
            pltpu.VMEM((n - 2, *shard), bf16),
            hops,
            hops,
            hops,
            hops,
            pltpu.SemaphoreType.DMA((2, n - 2, kv)),
        ],
        compiler_params=pltpu.CompilerParams(
            collective_id=0, has_side_effects=True, vmem_limit_bytes=60 * 2**20
        ),
    )(
        block_list,
        visible_count,
        queries,
        grad_output,
        key_states,
        value_states,
    )
    steps = 2
    wide_spec = pl.BlockSpec((tok // steps, *queries.shape[1:]), lambda i: (i, 0, 0))
    head_spec = pl.BlockSpec((kv, tok // steps, dim), lambda i: (0, i, 0))
    tok_spec = pl.BlockSpec((tok // steps, kv, dim), lambda i: (i, 0, 0))
    return pl.pallas_call(
        write_kernel,
        grid=(steps,),
        out_shape=(
            jax.ShapeDtypeStruct(queries.shape, bf16),
            jax.ShapeDtypeStruct(queries.shape, bf16),
            jax.ShapeDtypeStruct(key_states.shape, bf16),
            jax.ShapeDtypeStruct(key_states.shape, bf16),
        ),
        in_specs=[wide_spec, wide_spec, head_spec, head_spec],
        out_specs=(wide_spec, wide_spec, tok_spec, tok_spec),
    )(out, dq, dk, dv)


def pick_body(*args):
    n = lax.axis_size("seq")
    return short_body(*args) if n == 4 and args[1].shape[0] == 2 * BLOCK else body(*args)


def solution(mesh):
    return jax.shard_map(
        pick_body,
        mesh=mesh,
        in_specs=(
            P(("group", "seq"), "head", None),
            P(("group", "seq"), "head", None),
            P(("group", "seq"), "head", None),
            P(("group", "seq"), "head", None),
            P(("group", "seq"), None),
            P(("group", "seq")),
        ),
        out_specs=(
            P(("group", "seq"), "head", None),
            P(("group", "seq"), "head", None),
            P(("group", "seq"), "head", None),
            P(("group", "seq"), "head", None),
        ),
        check_vma=False,
    )
```

```python
from functools import partial
import math

import jax
import jax.numpy as jnp
from jax import lax
from jax.experimental import pallas as pl
from jax.experimental.pallas import tpu as pltpu
from jax.sharding import PartitionSpec as P

BLOCK = 128
REACH = 16
FAR = -1e30
CHUNK = 512


def from_behind(block, axis, distance):
    devices = range(lax.axis_size(axis))
    route = [(i - distance, i) for i in devices if i - distance in devices]
    return lax.ppermute(block, axis, route)


def pick_blocks(blocks, at):
    return jnp.concatenate(
        [lax.dynamic_slice_in_dim(blocks, at[s], 1, 0) for s in range(at.shape[0])], 0
    )


def block_step(carried, inputs, key_blocks, value_blocks, base_block, score_scale):
    grad_key_win, grad_value_win = carried
    block_index, query_blk, gradout_blk, picked, live_count = inputs
    local_blocks = picked - base_block
    key_sel = pick_blocks(key_blocks, local_blocks)
    value_sel = pick_blocks(value_blocks, local_blocks)
    positions = jnp.arange(query_blk.shape[0])
    causal = positions[None, :] <= positions[:, None]
    slot_live = jnp.arange(picked.shape[0]) < live_count
    diagonal = picked == block_index
    visible = slot_live[None, :, None] & (
        jnp.logical_not(diagonal)[None, :, None] | causal[:, None, :]
    )
    scores = (
        jnp.einsum("rhgd,skhd->hgrsk", query_blk, key_sel, preferred_element_type=jnp.float32)
        * score_scale
    )
    scores = jnp.where(visible, scores, -1e30)
    row_top = jnp.max(scores, axis=(3, 4), keepdims=True)
    weights = jnp.exp(scores - row_top)
    row_total = jnp.sum(weights, axis=(3, 4), keepdims=True)
    mixed_rows = jnp.einsum(
        "hgrsk,skhd->rhgd",
        weights.astype(jnp.bfloat16),
        value_sel,
        preferred_element_type=jnp.float32,
    )
    norm_total = jnp.transpose(row_total[:, :, :, 0, 0], (2, 0, 1))[..., None]
    out_blk = (mixed_rows / norm_total).astype(jnp.bfloat16)
    log_total = row_top + jnp.log(row_total)
    row_delta = jnp.sum(gradout_blk.astype(jnp.float32) * out_blk.astype(jnp.float32), axis=-1)
    row_delta = jnp.transpose(row_delta, (1, 2, 0))[..., None, None]
    prob_full = jnp.exp(scores - log_total)
    prob_bf = prob_full.astype(jnp.bfloat16)
    grad_prob = jnp.einsum(
        "rhgd,skhd->hgrsk", gradout_blk, value_sel, preferred_element_type=jnp.float32
    )
    grad_score = (prob_full * (grad_prob - row_delta)).astype(jnp.bfloat16)
    grad_query_blk = (
        jnp.einsum("hgrsk,skhd->rhgd", grad_score, key_sel, preferred_element_type=jnp.float32)
        * score_scale
    ).astype(jnp.bfloat16)
    key_part = (
        jnp.einsum("hgrsk,rhgd->skhd", grad_score, query_blk, preferred_element_type=jnp.float32)
        * score_scale
    )
    value_part = jnp.einsum(
        "hgrsk,rhgd->skhd", prob_bf, gradout_blk, preferred_element_type=jnp.float32
    )
    grad_key_win = grad_key_win.at[local_blocks].add(key_part)
    grad_value_win = grad_value_win.at[local_blocks].add(value_part)
    return ((grad_key_win, grad_value_win), (out_blk, grad_query_blk))


def body(queries, key_states, value_states, grad_output, block_list, visible_count):
    tok_dev, kv_dev, head_dim = key_states.shape
    q_dev = queries.shape[1]
    group_size = q_dev // kv_dev
    blocks_dev = tok_dev // BLOCK
    seq_size = lax.axis_size("seq")
    seq_index = lax.axis_index("seq")
    reachable = min(REACH, seq_size - 1)
    score_scale = 1.0 / math.sqrt(head_dim)
    key_parts = []
    value_parts = []
    for distance in range(REACH, 0, -1):
        if distance <= reachable:
            far_keys, far_values = from_behind((key_states, value_states), "seq", distance)
        else:
            far_keys = jnp.zeros_like(key_states)
            far_values = jnp.zeros_like(value_states)
        key_parts.append(far_keys)
        value_parts.append(far_values)
    key_window = jnp.concatenate(key_parts + [key_states], 0)
    value_window = jnp.concatenate(value_parts + [value_states], 0)
    key_blocks = key_window.reshape((REACH + 1) * blocks_dev, BLOCK, kv_dev, head_dim)
    value_blocks = value_window.reshape((REACH + 1) * blocks_dev, BLOCK, kv_dev, head_dim)
    base_block = (seq_index - REACH) * blocks_dev
    block_ids = seq_index * blocks_dev + jnp.arange(blocks_dev, dtype=jnp.int32)
    query_grid = queries.reshape(blocks_dev, BLOCK, kv_dev, group_size, head_dim)
    gradout_grid = grad_output.reshape(blocks_dev, BLOCK, kv_dev, group_size, head_dim)
    initial = (jnp.zeros(key_blocks.shape, jnp.float32), jnp.zeros(value_blocks.shape, jnp.float32))
    stepper = partial(
        block_step,
        key_blocks=key_blocks,
        value_blocks=value_blocks,
        base_block=base_block,
        score_scale=score_scale,
    )
    (grad_key_win, grad_value_win), (out_blocks, grad_query_blocks) = lax.scan(
        stepper, initial, (block_ids, query_grid, gradout_grid, block_list, visible_count)
    )
    attn_out = out_blocks.reshape(tok_dev, q_dev, head_dim)
    grad_queries = grad_query_blocks.reshape(tok_dev, q_dev, head_dim)
    key_segments = grad_key_win.reshape(REACH + 1, tok_dev, kv_dev, head_dim)
    value_segments = grad_value_win.reshape(REACH + 1, tok_dev, kv_dev, head_dim)
    grad_keys = key_segments[REACH]
    grad_values = value_segments[REACH]
    for distance in range(1, reachable + 1):
        back_keys, back_values = from_behind(
            (key_segments[REACH - distance], value_segments[REACH - distance]), "seq", -distance
        )
        grad_keys = grad_keys + back_keys
        grad_values = grad_values + back_values
    return (
        attn_out,
        grad_queries,
        grad_keys.astype(jnp.bfloat16),
        grad_values.astype(jnp.bfloat16),
    )


NT = (((1,), (1,)), ((), ()))
NN = (((1,), (0,)), ((), ()))


def dot(a, b, dims):
    return lax.dot_general(a, b, dims, preferred_element_type=jnp.float32)


def layer_kernel(
    n,
    list_ref,
    count_ref,
    q_in,
    do_in,
    k_in,
    v_in,
    out_ref,
    dq_ref,
    dk_ref,
    dv_ref,
    bias,
    q_ref,
    do_ref,
    k_raw,
    v_raw,
    io_sems,
    kall,
    vall,
    kt,
    vt,
    qs,
    dos,
    wide,
    prob,
    score_grad,
    tops,
    sums,
    factor,
    delta,
    out_t,
    dq_t,
    dk_own,
    dv_own,
    dk_send,
    dv_send,
    dk_recv,
    dv_recv,
    dv_mid,
    k_sems,
    v_sems,
    dk_sems,
    dv_sems,
    mid_sems,
):
    z = lax.axis_index("seq")
    last = n - 1
    barrier = pltpu.get_barrier_semaphore()

    @pl.when(z > 0)
    def _():
        pl.semaphore_signal(barrier, inc=1, device_id={"seq": z - 1})

    @pl.when(z < last)
    def _():
        pl.semaphore_signal(barrier, inc=1, device_id={"seq": z + 1})

    k_copy = pltpu.make_async_copy(k_in, k_raw, io_sems.at[0])
    v_copy = pltpu.make_async_copy(v_in, v_raw, io_sems.at[1])
    q_copy = pltpu.make_async_copy(q_in, q_ref, io_sems.at[2])
    do_copy = pltpu.make_async_copy(do_in, do_ref, io_sems.at[3])
    k_copy.start()
    q_copy.start()
    v_copy.start()
    do_copy.start()
    _, kv, tok, dim = kall.shape
    group = q_ref.shape[1] // kv
    blocks = tok // BLOCK
    rows = tok * group
    chunks = rows // CHUNK
    block_rows = BLOCK * group
    scale = 1.0 / math.sqrt(dim)
    scale2 = scale * math.log2(math.e)

    def hop(held, sems, h, d):
        return pltpu.make_async_remote_copy(
            src_ref=held.at[d, h],
            dst_ref=held.at[d + 1, h],
            send_sem=sems.at[0, d, h],
            recv_sem=sems.at[1, d, h],
            device_id={"seq": z + 1},
        )

    def k_hop(h, d):
        return hop(kall, k_sems, h, d)

    def v_hop(h, d):
        return hop(vall, v_sems, h, d)

    def back(send, recv, sems, h, d):
        return pltpu.make_async_remote_copy(
            src_ref=send.at[d - 1, h],
            dst_ref=recv.at[d - 1, h],
            send_sem=sems.at[0, d - 1, h],
            recv_sem=sems.at[1, d - 1, h],
            device_id={"seq": z - d},
        )

    def mid_back(h, d):
        return pltpu.make_async_remote_copy(
            src_ref=dv_send.at[d - 1, h],
            dst_ref=dv_mid.at[d - 2, h],
            send_sem=mid_sems.at[0, d - 2, h],
            recv_sem=mid_sems.at[1, d - 2, h],
            device_id={"seq": z - 1},
        )

    def dk_back(h, d):
        return back(dk_send, dk_recv, dk_sems, h, d)

    def dv_back(h, d):
        return back(dv_send, dv_recv, dv_sems, h, d)

    def split_heads(src, dst, dst_t):
        full = src[...].astype(jnp.float32)
        for h in range(kv):
            part = full[:, h, :]
            dst[0, h] = part.astype(jnp.bfloat16)

    for b in range(blocks):
        for d in range(n):
            for j in range(blocks):
                c = (z - d) * blocks + j
                hits = jnp.int32(0)
                for s in range(list_ref.shape[1]):
                    live = jnp.logical_and(list_ref[b, s] == c, s < count_ref[b])
                    hits = jnp.where(live, jnp.int32(1), hits)
                bias[b, d * blocks + j] = jnp.where(hits > 0, jnp.float32(0.0), jnp.float32(FAR))

    k_copy.wait()
    split_heads(k_raw, kall, kt)

    inner = jnp.logical_and(z > 0, z < last)

    @pl.when(inner)
    def _():
        pl.semaphore_wait(barrier, 2)

    @pl.when(jnp.logical_not(inner))
    def _():
        pl.semaphore_wait(barrier, 1)

    @pl.when(z < last)
    def _():
        k_hop(0, 0).start()

    @pl.when(z == 0)
    def _():
        k_hop(1, 0).start()

    v_copy.wait()
    split_heads(v_raw, vall, vt)

    tops[...] = jnp.full(tops.shape, FAR, jnp.float32)
    sums[...] = jnp.zeros(sums.shape, jnp.float32)
    delta[...] = jnp.zeros(delta.shape, jnp.float32)

    step_tok = CHUNK // group

    def regroup_from(src, dst):
        def step(i, _):
            at = pl.ds(pl.multiple_of(i * step_tok, step_tok), step_tok)
            to = pl.ds(pl.multiple_of(i * CHUNK, CHUNK), CHUNK)
            full = src[at].astype(jnp.float32)
            for h in range(kv):
                part = full[:, h * group : (h + 1) * group, :]
                dst[h, to, :] = part.reshape(CHUNK, dim).astype(jnp.bfloat16)
            return 0

        lax.fori_loop(0, tok // step_tok, step, 0)

    def lanes(c):
        return slice(c * CHUNK, (c + 1) * CHUNK)

    def keys_of(d):
        return slice(d * tok, (d + 1) * tok)

    def score_unit(h, d):
        keys = kall[d, h]
        for c in range(chunks):
            b = c * CHUNK // block_rows
            s = dot(keys, qs[h, lanes(c), :], NT) * scale2
            parts = []
            for j in range(blocks):
                sj = s[j * BLOCK : (j + 1) * BLOCK]
                if d == 0 and j > b:
                    sj = jnp.full(sj.shape, FAR, jnp.float32)
                elif d == 0 and j == b:
                    first = (c * CHUNK - b * block_rows) // group
                    p_at = lax.broadcasted_iota(jnp.int32, sj.shape, 0)
                    t_at = first + lax.broadcasted_iota(jnp.int32, sj.shape, 1) // group
                    sj = jnp.where(p_at <= t_at, sj, FAR)
                else:
                    sj = sj + bias[b, d * blocks + j]
                parts.append(sj)
            s = jnp.concatenate(parts, 0)
            top = jnp.max(s, axis=0, keepdims=True)
            w = jnp.exp2(s - top)
            tops[d, h, :, lanes(c)] = top
            sums[d, h, :, lanes(c)] = jnp.sum(w, axis=0, keepdims=True)
            wide[d, h, :, lanes(c)] = w

    def factors(h):
        top = tops[0, h]
        for d in range(1, n):
            top = jnp.maximum(top, tops[d, h])
        grow = [jnp.exp2(tops[d, h] - top) for d in range(n)]
        total = sum(grow[d] * sums[d, h] for d in range(n))
        for d in range(n):
            factor[d, h] = grow[d] / total

    def prob_unit(h, d):
        acc = jnp.zeros((tok, dim), jnp.float32)
        for c in range(chunks):
            p = (wide[d, h, :, lanes(c)] * factor[d, h, :, lanes(c)]).astype(jnp.bfloat16)
            prob[h, keys_of(d), lanes(c)] = p
            acc = acc + dot(p, dos[h, lanes(c), :], NN)
        return acc

    def value_unit(h, d):
        values = vall[d, h]
        vt[h, :, keys_of(d)] = values.astype(jnp.float32).T.astype(jnp.bfloat16)
        for c in range(chunks):
            p = prob[h, keys_of(d), lanes(c)]
            gp = dot(values, dos[h, lanes(c), :], NT)
            wide[d, h, :, lanes(c)] = gp
            delta[h, :, lanes(c)] += jnp.sum(p.astype(jnp.float32) * gp, axis=0, keepdims=True)

    def grad_unit(h, d):
        acc = jnp.zeros((tok, dim), jnp.float32)
        for c in range(chunks):
            p = prob[h, keys_of(d), lanes(c)].astype(jnp.float32)
            gs = p * (wide[d, h, :, lanes(c)] - delta[h, :, lanes(c)])
            gs = gs.astype(jnp.bfloat16)
            score_grad[h, keys_of(d), lanes(c)] = gs
            acc = acc + dot(gs, qs[h, lanes(c), :], NN)
        return acc * scale

    def mix_unit(h, left, right, dst, k):
        span = (k + 1) * tok
        for c in range(chunks):
            dst[h, :, lanes(c)] = dot(left[h, :, :span], right[h, :span, lanes(c)], NN)

    def arrive(hop_of, h, d, then):
        if d > 0:
            hop_of(h, d - 1).wait_recv()
        if 0 < d < last:

            @pl.when(z < last)
            def _():
                hop_of(h, d).start()

        if then is not None and d < last:

            @pl.when(z == d)
            def _():
                then()

    def score_head(h):
        for d in range(n):

            @pl.when(z >= d)
            def _(d=d):
                if h == 0 and d > 0:
                    arrive(k_hop, h, d, lambda: k_hop(1, 0).start())
                elif h == 1:
                    arrive(k_hop, h, d, lambda: v_hop(0, 0).start())
                score_unit(h, d)

        factors(h)

    def prob_head(h):
        for d in range(last, 0, -1):

            @pl.when(z >= d)
            def _(d=d):
                acc = prob_unit(h, d)

                @pl.when(z == last - 1)
                def _():
                    dv_own[d, h] = acc

                @pl.when(z != last - 1)
                def _():
                    dv_send[d - 1, h] = acc.astype(jnp.bfloat16)

                if d == 1:

                    @pl.when(z != last - 1)
                    def _():
                        dv_back(h, d).start()

                else:

                    @pl.when(z == last)
                    def _():
                        mid_back(h, d).start()

                    @pl.when(z < last - 1)
                    def _():
                        dv_back(h, d).start()

    def mid_head(h):
        @pl.when(z == last - 1)
        def _():
            for d in range(last - 1, 0, -1):
                mid_back(h, d + 1).wait_recv()
                both = dv_own[d, h] + dv_mid[d - 1, h].astype(jnp.float32)
                dv_send[d - 1, h] = both.astype(jnp.bfloat16)
                dv_back(h, d).start()

    def value_head(h):
        for d in range(n):

            @pl.when(z >= d)
            def _(d=d):
                if h == 0:
                    arrive(v_hop, h, d, lambda: v_hop(1, 0).start())
                else:
                    arrive(v_hop, h, d, None)
                value_unit(h, d)

    def grad_head(h):
        for d in range(last, 0, -1):

            @pl.when(z >= d)
            def _(d=d):
                dk_send[d - 1, h] = grad_unit(h, d).astype(jnp.bfloat16)
                dk_back(h, d).start()

    def mix_head(h, left, right, dst):
        for k in range(n):

            @pl.when(z == k)
            def _(k=k):
                mix_unit(h, left, right, dst, k)

    def key_turns(h):
        for d in range(n):

            @pl.when(z >= d)
            def _(d=d):
                kt[h, :, keys_of(d)] = kall[d, h].astype(jnp.float32).T.astype(jnp.bfloat16)

    q_copy.wait()
    regroup_from(q_ref, qs)
    score_head(0)
    do_copy.wait()
    regroup_from(do_ref, dos)
    prob_head(0)
    score_head(1)
    prob_head(1)
    for h in range(kv):
        dv_own[0, h] = prob_unit(h, 0)
    value_head(0)
    mid_head(0)
    grad_head(0)
    value_head(1)
    grad_head(1)
    mid_head(1)
    for h in range(kv):
        dk_own[0, h] = grad_unit(h, 0)

    def untwist(src, dst, factor_out):
        for i in range(tok // step_tok):
            heads = []
            for h in range(kv):
                x = src[h, :, i * CHUNK : (i + 1) * CHUNK].T
                heads.append(x.reshape(step_tok, group, dim))
            full = jnp.concatenate(heads, 1) * factor_out
            dst[i * step_tok : (i + 1) * step_tok] = full.astype(jnp.bfloat16)

    for h in range(kv):
        mix_head(h, vt, prob, out_t)
    untwist(out_t, out_ref, 1.0)
    for h in range(kv):
        key_turns(h)
        mix_head(h, kt, score_grad, dq_t)
    untwist(dq_t, dq_ref, scale)

    for e in range(1, n):

        @pl.when(z + e <= last)
        def _(e=e):
            for h in range(kv):

                @pl.when(jnp.logical_or(e == 1, z + e < last))
                def _():
                    dv_back(h, e).wait_recv()
                    dv_own[0, h] += dv_recv[e - 1, h].astype(jnp.float32)

                dk_back(h, e).wait_recv()
                dk_own[0, h] += dk_recv[e - 1, h].astype(jnp.float32)

    for own, dst in ((dv_own, dv_ref), (dk_own, dk_ref)):
        dst[...] = jnp.stack([own[0, h] for h in range(kv)], axis=1).astype(jnp.bfloat16)

    for d in range(n - 1):

        @pl.when(jnp.logical_and(z >= d, z < last))
        def _(d=d):
            for h in range(kv):
                k_hop(h, d).wait_send()
                v_hop(h, d).wait_send()

    for d in range(1, n):

        @pl.when(z >= d)
        def _(d=d):
            for h in range(kv):
                dk_back(h, d).wait_send()
                if d == 1:
                    dv_back(h, d).wait_send()
                else:

                    @pl.when(z == last)
                    def _():
                        mid_back(h, d).wait_send()

                    @pl.when(z < last)
                    def _():
                        dv_back(h, d).wait_send()


def write_kernel(out_in, dq_in, dk_in, dv_in, out_ref, dq_ref, dk_ref, dv_ref, sems):
    pairs = ((out_in, out_ref), (dq_in, dq_ref), (dk_in, dk_ref), (dv_in, dv_ref))
    copies = [pltpu.make_async_copy(a, b, sems.at[i]) for i, (a, b) in enumerate(pairs)]
    for copy in copies:
        copy.start()
    for copy in copies:
        copy.wait()


def short_body(queries, key_states, value_states, grad_output, block_list, visible_count):
    n = lax.axis_size("seq")
    tok, kv, dim = key_states.shape
    group = queries.shape[1] // kv
    rows = tok * group
    blocks = tok // BLOCK
    shard = (kv, tok, dim)
    vmem = pl.BlockSpec(memory_space=pltpu.VMEM)
    smem = pl.BlockSpec(memory_space=pltpu.SMEM)
    hbm = pl.BlockSpec(memory_space=pl.ANY)
    f32, bf16 = jnp.float32, jnp.bfloat16
    hops = pltpu.SemaphoreType.DMA((2, n - 1, kv))
    parts = pltpu.VMEM((n - 1, *shard), bf16)
    made = pl.pallas_call(
        partial(layer_kernel, n),
        out_shape=(
            pltpu.VMEM(queries.shape, bf16),
            pltpu.VMEM(queries.shape, bf16),
            pltpu.VMEM(key_states.shape, bf16),
            pltpu.VMEM(key_states.shape, bf16),
        ),
        in_specs=[smem, smem, hbm, hbm, hbm, hbm],
        out_specs=(vmem, vmem, vmem, vmem),
        scratch_shapes=[
            pltpu.SMEM((blocks, n * blocks), f32),
            pltpu.VMEM(queries.shape, bf16),
            pltpu.VMEM(queries.shape, bf16),
            pltpu.VMEM(key_states.shape, bf16),
            pltpu.VMEM(key_states.shape, bf16),
            pltpu.SemaphoreType.DMA((4,)),
            pltpu.VMEM((n, *shard), bf16),
            pltpu.VMEM((n, *shard), bf16),
            pltpu.VMEM((kv, dim, n * tok), bf16),
            pltpu.VMEM((kv, dim, n * tok), bf16),
            pltpu.VMEM((kv, rows, dim), bf16),
            pltpu.VMEM((kv, rows, dim), bf16),
            pltpu.VMEM((n, kv, tok, rows), f32),
            pltpu.VMEM((kv, n * tok, rows), bf16),
            pltpu.VMEM((kv, n * tok, rows), bf16),
            pltpu.VMEM((n, kv, 1, rows), f32),
            pltpu.VMEM((n, kv, 1, rows), f32),
            pltpu.VMEM((n, kv, 1, rows), f32),
            pltpu.VMEM((kv, 1, rows), f32),
            pltpu.VMEM((kv, dim, rows), f32),
            pltpu.VMEM((kv, dim, rows), f32),
            pltpu.VMEM((1, *shard), f32),
            pltpu.VMEM((n, *shard), f32),
            parts,
            parts,
            parts,
            parts,
            pltpu.VMEM((n - 2, *shard), bf16),
            hops,
            hops,
            hops,
            hops,
            pltpu.SemaphoreType.DMA((2, n - 2, kv)),
        ],
        compiler_params=pltpu.CompilerParams(
            collective_id=0, has_side_effects=True, vmem_limit_bytes=56 * 2**20
        ),
    )(
        block_list,
        visible_count,
        queries,
        grad_output,
        key_states,
        value_states,
    )
    made = [pltpu.with_memory_space_constraint(x, pltpu.VMEM) for x in made]
    return pl.pallas_call(
        write_kernel,
        out_shape=(
            jax.ShapeDtypeStruct(queries.shape, bf16),
            jax.ShapeDtypeStruct(queries.shape, bf16),
            jax.ShapeDtypeStruct(key_states.shape, bf16),
            jax.ShapeDtypeStruct(key_states.shape, bf16),
        ),
        in_specs=[vmem, vmem, vmem, vmem],
        out_specs=(hbm, hbm, hbm, hbm),
        scratch_shapes=[pltpu.SemaphoreType.DMA((4,))],
    )(*made)


def pick_body(*args):
    n = lax.axis_size("seq")
    return short_body(*args) if n == 4 and args[1].shape[0] == 2 * BLOCK else body(*args)


def solution(mesh):
    return jax.shard_map(
        pick_body,
        mesh=mesh,
        in_specs=(
            P(("group", "seq"), "head", None),
            P(("group", "seq"), "head", None),
            P(("group", "seq"), "head", None),
            P(("group", "seq"), "head", None),
            P(("group", "seq"), None),
            P(("group", "seq")),
        ),
        out_specs=(
            P(("group", "seq"), "head", None),
            P(("group", "seq"), "head", None),
            P(("group", "seq"), "head", None),
            P(("group", "seq"), "head", None),
        ),
        check_vma=False,
    )
```

```python
from functools import partial
import math

import jax
import jax.numpy as jnp
from jax import lax
from jax.experimental import pallas as pl
from jax.experimental.pallas import tpu as pltpu
from jax.sharding import PartitionSpec as P

BLOCK = 128
REACH = 16
FAR = -1e30
CHUNK = 512


def from_behind(block, axis, distance):
    devices = range(lax.axis_size(axis))
    route = [(i - distance, i) for i in devices if i - distance in devices]
    return lax.ppermute(block, axis, route)


def pick_blocks(blocks, at):
    return jnp.concatenate(
        [lax.dynamic_slice_in_dim(blocks, at[s], 1, 0) for s in range(at.shape[0])], 0
    )


def block_step(carried, inputs, key_blocks, value_blocks, base_block, score_scale):
    grad_key_win, grad_value_win = carried
    block_index, query_blk, gradout_blk, picked, live_count = inputs
    local_blocks = picked - base_block
    key_sel = pick_blocks(key_blocks, local_blocks)
    value_sel = pick_blocks(value_blocks, local_blocks)
    positions = jnp.arange(query_blk.shape[0])
    causal = positions[None, :] <= positions[:, None]
    slot_live = jnp.arange(picked.shape[0]) < live_count
    diagonal = picked == block_index
    visible = slot_live[None, :, None] & (
        jnp.logical_not(diagonal)[None, :, None] | causal[:, None, :]
    )
    scores = (
        jnp.einsum("rhgd,skhd->hgrsk", query_blk, key_sel, preferred_element_type=jnp.float32)
        * score_scale
    )
    scores = jnp.where(visible, scores, -1e30)
    row_top = jnp.max(scores, axis=(3, 4), keepdims=True)
    weights = jnp.exp(scores - row_top)
    row_total = jnp.sum(weights, axis=(3, 4), keepdims=True)
    mixed_rows = jnp.einsum(
        "hgrsk,skhd->rhgd",
        weights.astype(jnp.bfloat16),
        value_sel,
        preferred_element_type=jnp.float32,
    )
    norm_total = jnp.transpose(row_total[:, :, :, 0, 0], (2, 0, 1))[..., None]
    out_blk = (mixed_rows / norm_total).astype(jnp.bfloat16)
    log_total = row_top + jnp.log(row_total)
    row_delta = jnp.sum(gradout_blk.astype(jnp.float32) * out_blk.astype(jnp.float32), axis=-1)
    row_delta = jnp.transpose(row_delta, (1, 2, 0))[..., None, None]
    prob_full = jnp.exp(scores - log_total)
    prob_bf = prob_full.astype(jnp.bfloat16)
    grad_prob = jnp.einsum(
        "rhgd,skhd->hgrsk", gradout_blk, value_sel, preferred_element_type=jnp.float32
    )
    grad_score = (prob_full * (grad_prob - row_delta)).astype(jnp.bfloat16)
    grad_query_blk = (
        jnp.einsum("hgrsk,skhd->rhgd", grad_score, key_sel, preferred_element_type=jnp.float32)
        * score_scale
    ).astype(jnp.bfloat16)
    key_part = (
        jnp.einsum("hgrsk,rhgd->skhd", grad_score, query_blk, preferred_element_type=jnp.float32)
        * score_scale
    )
    value_part = jnp.einsum(
        "hgrsk,rhgd->skhd", prob_bf, gradout_blk, preferred_element_type=jnp.float32
    )
    grad_key_win = grad_key_win.at[local_blocks].add(key_part)
    grad_value_win = grad_value_win.at[local_blocks].add(value_part)
    return ((grad_key_win, grad_value_win), (out_blk, grad_query_blk))


def body(queries, key_states, value_states, grad_output, block_list, visible_count):
    tok_dev, kv_dev, head_dim = key_states.shape
    q_dev = queries.shape[1]
    group_size = q_dev // kv_dev
    blocks_dev = tok_dev // BLOCK
    seq_size = lax.axis_size("seq")
    seq_index = lax.axis_index("seq")
    reachable = min(REACH, seq_size - 1)
    score_scale = 1.0 / math.sqrt(head_dim)
    key_parts = []
    value_parts = []
    for distance in range(REACH, 0, -1):
        if distance <= reachable:
            far_keys, far_values = from_behind((key_states, value_states), "seq", distance)
        else:
            far_keys = jnp.zeros_like(key_states)
            far_values = jnp.zeros_like(value_states)
        key_parts.append(far_keys)
        value_parts.append(far_values)
    key_window = jnp.concatenate(key_parts + [key_states], 0)
    value_window = jnp.concatenate(value_parts + [value_states], 0)
    key_blocks = key_window.reshape((REACH + 1) * blocks_dev, BLOCK, kv_dev, head_dim)
    value_blocks = value_window.reshape((REACH + 1) * blocks_dev, BLOCK, kv_dev, head_dim)
    base_block = (seq_index - REACH) * blocks_dev
    block_ids = seq_index * blocks_dev + jnp.arange(blocks_dev, dtype=jnp.int32)
    query_grid = queries.reshape(blocks_dev, BLOCK, kv_dev, group_size, head_dim)
    gradout_grid = grad_output.reshape(blocks_dev, BLOCK, kv_dev, group_size, head_dim)
    initial = (jnp.zeros(key_blocks.shape, jnp.float32), jnp.zeros(value_blocks.shape, jnp.float32))
    stepper = partial(
        block_step,
        key_blocks=key_blocks,
        value_blocks=value_blocks,
        base_block=base_block,
        score_scale=score_scale,
    )
    (grad_key_win, grad_value_win), (out_blocks, grad_query_blocks) = lax.scan(
        stepper, initial, (block_ids, query_grid, gradout_grid, block_list, visible_count)
    )
    attn_out = out_blocks.reshape(tok_dev, q_dev, head_dim)
    grad_queries = grad_query_blocks.reshape(tok_dev, q_dev, head_dim)
    key_segments = grad_key_win.reshape(REACH + 1, tok_dev, kv_dev, head_dim)
    value_segments = grad_value_win.reshape(REACH + 1, tok_dev, kv_dev, head_dim)
    grad_keys = key_segments[REACH]
    grad_values = value_segments[REACH]
    for distance in range(1, reachable + 1):
        back_keys, back_values = from_behind(
            (key_segments[REACH - distance], value_segments[REACH - distance]), "seq", -distance
        )
        grad_keys = grad_keys + back_keys
        grad_values = grad_values + back_values
    return (
        attn_out,
        grad_queries,
        grad_keys.astype(jnp.bfloat16),
        grad_values.astype(jnp.bfloat16),
    )


NT = (((1,), (1,)), ((), ()))
NN = (((1,), (0,)), ((), ()))


def dot(a, b, dims):
    return lax.dot_general(a, b, dims, preferred_element_type=jnp.float32)


def layer_kernel(
    n,
    list_ref,
    count_ref,
    q_in,
    do_in,
    k_in,
    v_in,
    out_ref,
    dq_ref,
    dk_ref,
    dv_ref,
    bias,
    q_ref,
    do_ref,
    k_raw,
    v_raw,
    io_sems,
    kall,
    vall,
    kt,
    vt,
    qs,
    dos,
    wide,
    prob,
    score_grad,
    tops,
    sums,
    factor,
    delta,
    out_t,
    dq_t,
    dk_own,
    dv_own,
    dk_send,
    dv_send,
    dk_recv,
    dv_recv,
    dv_mid,
    k_sems,
    v_sems,
    dk_sems,
    dv_sems,
    mid_sems,
):
    z = lax.axis_index("seq")
    last = n - 1
    barrier = pltpu.get_barrier_semaphore()

    @pl.when(z > 0)
    def _():
        pl.semaphore_signal(barrier, inc=1, device_id={"seq": z - 1})

    @pl.when(z < last)
    def _():
        pl.semaphore_signal(barrier, inc=1, device_id={"seq": z + 1})

    k_copy = pltpu.make_async_copy(k_in, k_raw, io_sems.at[0])
    v_copy = pltpu.make_async_copy(v_in, v_raw, io_sems.at[1])
    q_copy = pltpu.make_async_copy(q_in, q_ref, io_sems.at[2])
    do_copy = pltpu.make_async_copy(do_in, do_ref, io_sems.at[3])
    k_copy.start()
    q_copy.start()
    v_copy.start()
    do_copy.start()
    _, kv, tok, dim = kall.shape
    group = q_ref.shape[1] // kv
    blocks = tok // BLOCK
    rows = tok * group
    chunks = rows // CHUNK
    block_rows = BLOCK * group
    scale = 1.0 / math.sqrt(dim)
    scale2 = scale * math.log2(math.e)

    def hop(held, sems, h, d):
        return pltpu.make_async_remote_copy(
            src_ref=held.at[d, h],
            dst_ref=held.at[d + 1, h],
            send_sem=sems.at[0, d, h],
            recv_sem=sems.at[1, d, h],
            device_id={"seq": z + 1},
        )

    def k_hop(h, d):
        return hop(kall, k_sems, h, d)

    def v_hop(h, d):
        return hop(vall, v_sems, h, d)

    def back(send, recv, sems, h, d):
        return pltpu.make_async_remote_copy(
            src_ref=send.at[d - 1, h],
            dst_ref=recv.at[d - 1, h],
            send_sem=sems.at[0, d - 1, h],
            recv_sem=sems.at[1, d - 1, h],
            device_id={"seq": z - d},
        )

    def mid_back(h, d):
        return pltpu.make_async_remote_copy(
            src_ref=dv_send.at[d - 1, h],
            dst_ref=dv_mid.at[d - 2, h],
            send_sem=mid_sems.at[0, d - 2, h],
            recv_sem=mid_sems.at[1, d - 2, h],
            device_id={"seq": z - 1},
        )

    def dk_back(h, d):
        return back(dk_send, dk_recv, dk_sems, h, d)

    def dv_back(h, d):
        return back(dv_send, dv_recv, dv_sems, h, d)

    def split_heads(src, dst, dst_t):
        full = src[...].astype(jnp.float32)
        for h in range(kv):
            part = full[:, h, :]
            dst[0, h] = part.astype(jnp.bfloat16)

    for b in range(blocks):
        for d in range(n):
            for j in range(blocks):
                c = (z - d) * blocks + j
                hits = jnp.int32(0)
                for s in range(list_ref.shape[1]):
                    live = jnp.logical_and(list_ref[b, s] == c, s < count_ref[b])
                    hits = jnp.where(live, jnp.int32(1), hits)
                bias[b, d * blocks + j] = jnp.where(hits > 0, jnp.float32(0.0), jnp.float32(FAR))

    k_copy.wait()
    split_heads(k_raw, kall, kt)

    inner = jnp.logical_and(z > 0, z < last)

    @pl.when(inner)
    def _():
        pl.semaphore_wait(barrier, 2)

    @pl.when(jnp.logical_not(inner))
    def _():
        pl.semaphore_wait(barrier, 1)

    @pl.when(z < last)
    def _():
        k_hop(0, 0).start()

    @pl.when(z == 0)
    def _():
        k_hop(1, 0).start()

    v_copy.wait()
    split_heads(v_raw, vall, vt)

    tops[...] = jnp.full(tops.shape, FAR, jnp.float32)
    sums[...] = jnp.zeros(sums.shape, jnp.float32)
    delta[...] = jnp.zeros(delta.shape, jnp.float32)

    step_tok = CHUNK // group

    def regroup_from(src, dst):
        def step(i, _):
            at = pl.ds(pl.multiple_of(i * step_tok, step_tok), step_tok)
            to = pl.ds(pl.multiple_of(i * CHUNK, CHUNK), CHUNK)
            full = src[at].astype(jnp.float32)
            for h in range(kv):
                part = full[:, h * group : (h + 1) * group, :]
                dst[h, to, :] = part.reshape(CHUNK, dim).astype(jnp.bfloat16)
            return 0

        lax.fori_loop(0, tok // step_tok, step, 0)

    def lanes(c):
        return slice(c * CHUNK, (c + 1) * CHUNK)

    def keys_of(d):
        return slice(d * tok, (d + 1) * tok)

    def score_unit(h, d):
        keys = kall[d, h]
        for c in range(chunks):
            b = c * CHUNK // block_rows
            s = dot(keys, qs[h, lanes(c), :], NT) * scale2
            parts = []
            for j in range(blocks):
                sj = s[j * BLOCK : (j + 1) * BLOCK]
                if d == 0 and j > b:
                    sj = jnp.full(sj.shape, FAR, jnp.float32)
                elif d == 0 and j == b:
                    first = (c * CHUNK - b * block_rows) // group
                    p_at = lax.broadcasted_iota(jnp.int32, sj.shape, 0)
                    t_at = first + lax.broadcasted_iota(jnp.int32, sj.shape, 1) // group
                    sj = jnp.where(p_at <= t_at, sj, FAR)
                else:
                    sj = sj + bias[b, d * blocks + j]
                parts.append(sj)
            s = jnp.concatenate(parts, 0)
            top = jnp.max(s, axis=0, keepdims=True)
            w = jnp.exp2(s - top)
            tops[d, h, :, lanes(c)] = top
            sums[d, h, :, lanes(c)] = jnp.sum(w, axis=0, keepdims=True)
            wide[d, h, :, lanes(c)] = w

    def factors(h):
        top = tops[0, h]
        for d in range(1, n):
            top = jnp.maximum(top, tops[d, h])
        grow = [jnp.exp2(tops[d, h] - top) for d in range(n)]
        total = sum(grow[d] * sums[d, h] for d in range(n))
        for d in range(n):
            factor[d, h] = grow[d] / total

    def prob_unit(h, d):
        acc = jnp.zeros((tok, dim), jnp.float32)
        for c in range(chunks):
            p = (wide[d, h, :, lanes(c)] * factor[d, h, :, lanes(c)]).astype(jnp.bfloat16)
            prob[h, keys_of(d), lanes(c)] = p
            acc = acc + dot(p, dos[h, lanes(c), :], NN)
        return acc

    def value_unit(h, d):
        values = vall[d, h]
        vt[h, :, keys_of(d)] = values.astype(jnp.float32).T.astype(jnp.bfloat16)
        for c in range(chunks):
            p = prob[h, keys_of(d), lanes(c)]
            gp = dot(values, dos[h, lanes(c), :], NT)
            wide[d, h, :, lanes(c)] = gp
            delta[h, :, lanes(c)] += jnp.sum(p.astype(jnp.float32) * gp, axis=0, keepdims=True)

    def grad_unit(h, d):
        acc = jnp.zeros((tok, dim), jnp.float32)
        for c in range(chunks):
            p = prob[h, keys_of(d), lanes(c)].astype(jnp.float32)
            gs = p * (wide[d, h, :, lanes(c)] - delta[h, :, lanes(c)])
            gs = gs.astype(jnp.bfloat16)
            score_grad[h, keys_of(d), lanes(c)] = gs
            acc = acc + dot(gs, qs[h, lanes(c), :], NN)
        return acc * scale

    def mix_unit(h, left, right, dst, k):
        span = (k + 1) * tok
        for c in range(chunks):
            dst[h, :, lanes(c)] = dot(left[h, :, :span], right[h, :span, lanes(c)], NN)

    def arrive(hop_of, h, d, then):
        if d > 0:
            hop_of(h, d - 1).wait_recv()
        if 0 < d < last:

            @pl.when(z < last)
            def _():
                hop_of(h, d).start()

        if then is not None and d < last:

            @pl.when(z == d)
            def _():
                then()

    def score_head(h):
        for d in range(n):

            @pl.when(z >= d)
            def _(d=d):
                if h == 0 and d > 0:
                    arrive(k_hop, h, d, lambda: k_hop(1, 0).start())
                elif h == 1:
                    arrive(k_hop, h, d, lambda: v_hop(0, 0).start())
                score_unit(h, d)

        factors(h)

    def prob_head(h):
        for d in range(last, 0, -1):

            @pl.when(z >= d)
            def _(d=d):
                acc = prob_unit(h, d)

                @pl.when(z == last - 1)
                def _():
                    dv_own[d, h] = acc

                @pl.when(z != last - 1)
                def _():
                    dv_send[d - 1, h] = acc.astype(jnp.bfloat16)

                if d == 1:

                    @pl.when(z != last - 1)
                    def _():
                        dv_back(h, d).start()

                else:

                    @pl.when(z == last)
                    def _():
                        mid_back(h, d).start()

                    @pl.when(z < last - 1)
                    def _():
                        dv_back(h, d).start()

    def mid_head(h):
        @pl.when(z == last - 1)
        def _():
            for d in range(last - 1, 0, -1):
                mid_back(h, d + 1).wait_recv()
                both = dv_own[d, h] + dv_mid[d - 1, h].astype(jnp.float32)
                dv_send[d - 1, h] = both.astype(jnp.bfloat16)
                dv_back(h, d).start()

    def value_head(h):
        for d in range(n):

            @pl.when(z >= d)
            def _(d=d):
                if h == 0:
                    arrive(v_hop, h, d, lambda: v_hop(1, 0).start())
                elif d > 0:

                    @pl.when(z == last)
                    def _():
                        v_hop(h, d - 1).wait_recv()

                value_unit(h, d)

    def pass_values(h):
        for d in range(1, last):

            @pl.when(jnp.logical_and(z >= d, z < last))
            def _(d=d):
                arrive(v_hop, h, d, None)

    def grad_head(h):
        for d in range(last, 0, -1):

            @pl.when(z >= d)
            def _(d=d):
                dk_send[d - 1, h] = grad_unit(h, d).astype(jnp.bfloat16)
                dk_back(h, d).start()

    def mix_head(h, left, right, dst):
        for k in range(n):

            @pl.when(z == k)
            def _(k=k):
                mix_unit(h, left, right, dst, k)

    def key_turns(h):
        for d in range(n):

            @pl.when(z >= d)
            def _(d=d):
                kt[h, :, keys_of(d)] = kall[d, h].astype(jnp.float32).T.astype(jnp.bfloat16)

    q_copy.wait()
    regroup_from(q_ref, qs)
    score_head(0)
    do_copy.wait()
    regroup_from(do_ref, dos)
    prob_head(0)
    score_head(1)
    prob_head(1)
    for h in range(kv):
        dv_own[0, h] = prob_unit(h, 0)
    value_head(0)
    pass_values(1)
    mid_head(0)
    grad_head(0)
    value_head(1)
    grad_head(1)
    mid_head(1)
    for h in range(kv):
        dk_own[0, h] = grad_unit(h, 0)

    def untwist(src, dst, factor_out):
        for i in range(tok // step_tok):
            heads = []
            for h in range(kv):
                x = src[h, :, i * CHUNK : (i + 1) * CHUNK].T
                heads.append(x.reshape(step_tok, group, dim))
            full = jnp.concatenate(heads, 1) * factor_out
            dst[i * step_tok : (i + 1) * step_tok] = full.astype(jnp.bfloat16)

    for h in range(kv):
        mix_head(h, vt, prob, out_t)
    untwist(out_t, out_ref, 1.0)
    for h in range(kv):
        key_turns(h)
        mix_head(h, kt, score_grad, dq_t)
    untwist(dq_t, dq_ref, scale)

    for e in range(1, n):

        @pl.when(z + e <= last)
        def _(e=e):
            for h in range(kv):

                @pl.when(jnp.logical_or(e == 1, z + e < last))
                def _():
                    dv_back(h, e).wait_recv()
                    dv_own[0, h] += dv_recv[e - 1, h].astype(jnp.float32)

                dk_back(h, e).wait_recv()
                dk_own[0, h] += dk_recv[e - 1, h].astype(jnp.float32)

    for own, dst in ((dv_own, dv_ref), (dk_own, dk_ref)):
        dst[...] = jnp.stack([own[0, h] for h in range(kv)], axis=1).astype(jnp.bfloat16)

    for d in range(n - 1):

        @pl.when(jnp.logical_and(z >= d, z < last))
        def _(d=d):
            for h in range(kv):
                k_hop(h, d).wait_send()
                v_hop(h, d).wait_send()

    for d in range(1, n):

        @pl.when(z >= d)
        def _(d=d):
            for h in range(kv):
                dk_back(h, d).wait_send()
                if d == 1:
                    dv_back(h, d).wait_send()
                else:

                    @pl.when(z == last)
                    def _():
                        mid_back(h, d).wait_send()

                    @pl.when(z < last)
                    def _():
                        dv_back(h, d).wait_send()


def write_kernel(out_in, dq_in, dk_in, dv_in, out_ref, dq_ref, dk_ref, dv_ref, sems):
    pairs = ((out_in, out_ref), (dq_in, dq_ref), (dk_in, dk_ref), (dv_in, dv_ref))
    copies = [pltpu.make_async_copy(a, b, sems.at[i]) for i, (a, b) in enumerate(pairs)]
    for copy in copies:
        copy.start()
    for copy in copies:
        copy.wait()


def short_body(queries, key_states, value_states, grad_output, block_list, visible_count):
    n = lax.axis_size("seq")
    tok, kv, dim = key_states.shape
    group = queries.shape[1] // kv
    rows = tok * group
    blocks = tok // BLOCK
    shard = (kv, tok, dim)
    vmem = pl.BlockSpec(memory_space=pltpu.VMEM)
    smem = pl.BlockSpec(memory_space=pltpu.SMEM)
    hbm = pl.BlockSpec(memory_space=pl.ANY)
    f32, bf16 = jnp.float32, jnp.bfloat16
    hops = pltpu.SemaphoreType.DMA((2, n - 1, kv))
    parts = pltpu.VMEM((n - 1, *shard), bf16)
    made = pl.pallas_call(
        partial(layer_kernel, n),
        out_shape=(
            pltpu.VMEM(queries.shape, bf16),
            pltpu.VMEM(queries.shape, bf16),
            pltpu.VMEM(key_states.shape, bf16),
            pltpu.VMEM(key_states.shape, bf16),
        ),
        in_specs=[smem, smem, hbm, hbm, hbm, hbm],
        out_specs=(vmem, vmem, vmem, vmem),
        scratch_shapes=[
            pltpu.SMEM((blocks, n * blocks), f32),
            pltpu.VMEM(queries.shape, bf16),
            pltpu.VMEM(queries.shape, bf16),
            pltpu.VMEM(key_states.shape, bf16),
            pltpu.VMEM(key_states.shape, bf16),
            pltpu.SemaphoreType.DMA((4,)),
            pltpu.VMEM((n, *shard), bf16),
            pltpu.VMEM((n, *shard), bf16),
            pltpu.VMEM((kv, dim, n * tok), bf16),
            pltpu.VMEM((kv, dim, n * tok), bf16),
            pltpu.VMEM((kv, rows, dim), bf16),
            pltpu.VMEM((kv, rows, dim), bf16),
            pltpu.VMEM((n, kv, tok, rows), f32),
            pltpu.VMEM((kv, n * tok, rows), bf16),
            pltpu.VMEM((kv, n * tok, rows), bf16),
            pltpu.VMEM((n, kv, 1, rows), f32),
            pltpu.VMEM((n, kv, 1, rows), f32),
            pltpu.VMEM((n, kv, 1, rows), f32),
            pltpu.VMEM((kv, 1, rows), f32),
            pltpu.VMEM((kv, dim, rows), f32),
            pltpu.VMEM((kv, dim, rows), f32),
            pltpu.VMEM((1, *shard), f32),
            pltpu.VMEM((n, *shard), f32),
            parts,
            parts,
            parts,
            parts,
            pltpu.VMEM((n - 2, *shard), bf16),
            hops,
            hops,
            hops,
            hops,
            pltpu.SemaphoreType.DMA((2, n - 2, kv)),
        ],
        compiler_params=pltpu.CompilerParams(
            collective_id=0, has_side_effects=True, vmem_limit_bytes=56 * 2**20
        ),
    )(
        block_list,
        visible_count,
        queries,
        grad_output,
        key_states,
        value_states,
    )
    made = [pltpu.with_memory_space_constraint(x, pltpu.VMEM) for x in made]
    return pl.pallas_call(
        write_kernel,
        out_shape=(
            jax.ShapeDtypeStruct(queries.shape, bf16),
            jax.ShapeDtypeStruct(queries.shape, bf16),
            jax.ShapeDtypeStruct(key_states.shape, bf16),
            jax.ShapeDtypeStruct(key_states.shape, bf16),
        ),
        in_specs=[vmem, vmem, vmem, vmem],
        out_specs=(hbm, hbm, hbm, hbm),
        scratch_shapes=[pltpu.SemaphoreType.DMA((4,))],
    )(*made)


def pick_body(*args):
    n = lax.axis_size("seq")
    return short_body(*args) if n == 4 and args[1].shape[0] == 2 * BLOCK else body(*args)


def solution(mesh):
    return jax.shard_map(
        pick_body,
        mesh=mesh,
        in_specs=(
            P(("group", "seq"), "head", None),
            P(("group", "seq"), "head", None),
            P(("group", "seq"), "head", None),
            P(("group", "seq"), "head", None),
            P(("group", "seq"), None),
            P(("group", "seq")),
        ),
        out_specs=(
            P(("group", "seq"), "head", None),
            P(("group", "seq"), "head", None),
            P(("group", "seq"), "head", None),
            P(("group", "seq"), "head", None),
        ),
        check_vma=False,
    )
```
